256 devices in a mesh: ta: 4 (over y), ha: 16 (over x, z_hi, core), wa: 4 (over z_lo).
Axes of the slice: x: 4, y: 4, z: 8 (z_hi: 2, z_lo: 4; z = z_hi * 4 + z_lo), core: 2. Of those that a mesh axis runs over, the one named last changes fastest.
Arguments:
- latents: bfloat16 [8, 256, 128, 256], P('ta', 'ha', 'wa'), may hold values from -6 to 6
- norm_gain: float32 [256], replicated, may hold values from 0.1 to 1.9
- conv_weight: bfloat16 [3, 3, 3, 256, 256], replicated, may hold values from -0.078125 to 0.078125
- qkv_weight: bfloat16 [1024, 16, 3, 128], P(None, ('ta', 'wa')), may hold values from -2.7 to 2.7
Outputs:
- block_out: bfloat16 [8, 256, 128, 256], P('ta', 'ha', 'wa')
- attended: bfloat16 [8, 128, 64, 16, 128], P(None, 'ha', None, ('ta', 'wa'))
The draws below stay inside these ranges and needn't reach their ends.
All inputs are finite; a program needn't handle non-finite values.
Results may differ from the reference program's by a relative error of at most 0.0062.
Values may be sent and summed in bfloat16 or wider, within the bound.
No kernel may reach another device: no remote copies, remote signals or barrier semaphores. Data moves between devices by JAX's collectives and lax.ppermute only.
A program may use at most 128 MiB of HBM per device.

```python
import jax
import jax.numpy as jnp
from jax import lax

C = 256
HD = 128
WIN = 4
HEADS = 16
PD = 1024
NT = 8
NH = 256
NW = 128
PR = 128
PC = 64


def draw_qkv_weight(key, part):
    base = jax.random.truncated_normal(key, -6.0, 6.0, (PD, HEADS, 3, HD), jnp.float32) / PD ** 0.5
    return base.astype(jnp.bfloat16)


def block_scale(stream_key, shape, pieces, smallest, high):
    def one(dim, shards_of):
        steps = jax.random.uniform(jax.random.fold_in(jax.random.fold_in(stream_key, 6), dim), (shards_of,), jnp.float32, smallest / len(pieces), high / len(pieces))
        return jnp.repeat(jnp.exp(steps), shape[dim] // shards_of).reshape((-1,) + (1,) * (len(shape) - dim - 1))

    factor_of = one(*pieces[0])
    for cut in pieces[1:]:
        factor_of = factor_of * one(*cut)
    return factor_of


def gaussian(own_key, shape, width, limit, shards=(), held_as=jnp.bfloat16):
    entries = width * jax.random.normal(own_key, shape, jnp.float32)
    if shards:
        entries = entries * block_scale(own_key, shape, shards, -0.22, 0.18)
    return jnp.clip(entries, -limit, limit).astype(held_as)


def setup_inputs(seed: int = 0) -> dict:
    arg_keys = jax.random.split(jax.random.key(seed), 5)
    latents = gaussian(arg_keys[0], (NT, NH, NW, C), 1.0, 6.0, ((0, 4), (1, 16), (2, 4)))
    norm_gain = jnp.clip(1.0 + 0.18 * jax.random.normal(arg_keys[1], (C,), jnp.float32), 0.1, 1.9)
    conv_weight = gaussian(arg_keys[2], (3, 3, 3, C, C), (27 * C) ** -0.5, 0.078125)
    qkv_weight = draw_qkv_weight(jax.random.fold_in(arg_keys[4], 71), 0)
    return dict(latents=latents, norm_gain=norm_gain, conv_weight=conv_weight, qkv_weight=qkv_weight)


def reference(latents, norm_gain, conv_weight, qkv_weight):
    latent_f32 = latents.astype(jnp.float32)
    scale_rms = lax.rsqrt(lax.optimization_barrier(jnp.mean(latent_f32 * latent_f32, axis=-1, keepdims=True)) + 1e-06)
    normed = jax.nn.silu(latent_f32 * scale_rms * norm_gain).astype(jnp.bfloat16)
    conv_out = lax.conv_general_dilated(normed.astype(jnp.float32)[None], conv_weight.astype(jnp.float32), (1, 1, 1), 'SAME', dimension_numbers=('NDHWC', 'DHWIO', 'NDHWC'), precision=lax.Precision.HIGHEST)[0]
    block_out = (latent_f32 + conv_out).astype(jnp.bfloat16)
    patches = block_out.reshape(NT, PR, 2, PC, 2, C).transpose(0, 1, 3, 2, 4, 5).reshape(NT * PR * PC, PD).astype(jnp.float32)
    band_count = PR // WIN
    offsets = jnp.arange(3 * WIN, dtype=jnp.int32) - WIN
    q_row = jnp.arange(WIN, dtype=jnp.int32)[:, None]
    band_rows = jnp.arange(band_count, dtype=jnp.int32)[:, None, None] * WIN + offsets[None, None, :]
    allowed = (jnp.abs(q_row - offsets[None, :]) <= WIN)[None] & (band_rows >= 0) & (band_rows < PR)
    gather_rows = (jnp.arange(band_count, dtype=jnp.int32)[:, None] * WIN + jnp.arange(3 * WIN, dtype=jnp.int32)[None, :]).astype(jnp.int32)

    def one_head(head_weight):
        qkv_rows = jnp.dot(patches, head_weight.reshape(PD, 3 * HD).astype(jnp.float32), precision=lax.Precision.HIGHEST).astype(jnp.bfloat16)
        qkv_rows = lax.optimization_barrier(qkv_rows).astype(jnp.float32).reshape(NT, PR, PC, 3, HD)
        queries = qkv_rows[:, :, :, 0].reshape(NT, band_count, WIN, PC, HD)
        padded = jnp.pad(qkv_rows[:, :, :, 1:], ((0, 0), (WIN, WIN), (0, 0), (0, 0), (0, 0)))
        banded = jnp.take(padded, gather_rows, axis=1)
        scores = jnp.einsum('tniad,tnjbd->tniajb', queries, banded[..., 0, :], precision=lax.Precision.HIGHEST) * HD ** (-0.5)
        scores = jnp.where(allowed[None, :, :, None, :, None], scores, -1e+30)
        row_max = lax.optimization_barrier(jnp.max(scores, axis=(4, 5), keepdims=True))
        exp_scores = jnp.exp(scores - row_max)
        probs = (exp_scores / lax.optimization_barrier(jnp.sum(exp_scores, axis=(4, 5), keepdims=True))).astype(jnp.bfloat16)
        probs = lax.optimization_barrier(probs).astype(jnp.float32)
        result = jnp.einsum('tniajb,tnjbd->tniad', probs, banded[..., 1, :], precision=lax.Precision.HIGHEST)
        return result.astype(jnp.bfloat16).reshape(NT, PR, PC, HD)
    heads_out = lax.map(one_head, qkv_weight.transpose(1, 0, 2, 3))
    attended = heads_out.transpose(1, 2, 3, 0, 4)
    return (block_out, attended)
```

```python
import jax
import jax.numpy as jnp
from jax import lax
from jax.sharding import PartitionSpec as P

WIN = 4


def extended(cells, sides, width):
    for axis, dim in sides:
        count = lax.axis_size(axis)
        ends = count - 1
        head = lax.slice_in_dim(cells, 0, width, axis=dim)
        tail = lax.slice_in_dim(cells, cells.shape[dim] - width, cells.shape[dim], axis=dim)
        cells = jnp.concatenate(
            [
                lax.ppermute(tail, axis, [(i, (i + 1) % count) for i in range(ends)]),
                cells,
                lax.ppermute(head, axis, [((i + 1) % count, i) for i in range(ends)]),
            ],
            axis=dim,
        )
    return cells


def local(latents, norm_gain, conv_weight, qkv_weight):
    t_dev, h_dev, w_dev, channels = latents.shape
    rows_dev = h_dev // 2
    cols_dev = w_dev // 2
    latent_f32 = latents.astype(jnp.float32)
    scale_rms = lax.rsqrt(jnp.mean(latent_f32 * latent_f32, axis=-1, keepdims=True) + 1e-06)
    normed = jax.nn.silu(latent_f32 * scale_rms * norm_gain).astype(jnp.bfloat16)
    padded = extended(normed, (("ta", 0), ("ha", 1), ("wa", 2)), 1)
    conv_out = lax.conv_general_dilated(
        padded[None],
        conv_weight,
        (1, 1, 1),
        "VALID",
        dimension_numbers=("NDHWC", "DHWIO", "NDHWC"),
        preferred_element_type=jnp.float32,
    )[0]
    block_out = (latent_f32 + conv_out).astype(jnp.bfloat16)
    width_in, head_dev, qkv_count, head_size = qkv_weight.shape
    col_heads = lax.all_gather(qkv_weight, "ta", axis=1, tiled=True)
    heads = col_heads.shape[1]
    wide = lax.all_gather(block_out, "wa", axis=2, tiled=True)
    patch_cols = wide.shape[2] // 2
    patches = (
        wide.reshape(t_dev, rows_dev, 2, patch_cols, 2, channels)
        .transpose(0, 1, 3, 2, 4, 5)
        .reshape(t_dev * rows_dev * patch_cols, 4 * channels)
    )
    projected = jnp.dot(
        patches, col_heads.reshape(width_in, -1), preferred_element_type=jnp.float32
    ).astype(jnp.bfloat16)
    qkv_rows = projected.reshape(t_dev, rows_dev, patch_cols, heads, qkv_count, head_size)
    queries = qkv_rows[:, :, :, :, 0, :]
    key_value = qkv_rows[:, :, :, :, 1:, :].reshape(
        t_dev, rows_dev, patch_cols, heads, 2 * head_size
    )
    kv_rim = extended(key_value, (("ha", 1),), WIN)
    row_base = lax.axis_index("ha") * rows_dev
    total_rows = rows_dev * lax.axis_size("ha")

    def attend(block_idx):
        q_block = lax.dynamic_slice_in_dim(queries, block_idx * WIN, WIN, 1)
        kv_block = lax.dynamic_slice_in_dim(kv_rim, block_idx * WIN, 3 * WIN, 1)
        key_part = kv_block[..., :head_size]
        value_part = kv_block[..., head_size:]
        scores = jnp.einsum(
            "tiahd,tjbhd->thiajb", q_block, key_part, preferred_element_type=jnp.float32
        ) * head_size ** (-0.5)
        q_row = jnp.arange(WIN, dtype=jnp.int32)[:, None]
        k_row = jnp.arange(3 * WIN, dtype=jnp.int32)[None, :] - WIN
        k_global = row_base + block_idx * WIN + k_row
        allowed = (jnp.abs(q_row - k_row) <= WIN) & (k_global >= 0) & (k_global < total_rows)
        scores = jnp.where(allowed[None, None, :, None, :, None], scores, -1e30)
        row_max = jnp.max(scores, axis=(4, 5), keepdims=True)
        exp_scores = jnp.exp(scores - row_max)
        probs = (exp_scores / jnp.sum(exp_scores, axis=(4, 5), keepdims=True)).astype(jnp.bfloat16)
        result = jnp.einsum(
            "thiajb,tjbhd->tiahd", probs, value_part, preferred_element_type=jnp.float32
        )
        return result.astype(jnp.bfloat16)

    blocks = lax.map(attend, jnp.arange(rows_dev // WIN, dtype=jnp.int32))
    attended = blocks.transpose(1, 0, 2, 3, 4, 5).reshape(
        t_dev, rows_dev, patch_cols, heads, head_size
    )
    attended = lax.all_to_all(attended, "ta", split_axis=3, concat_axis=0, tiled=True)
    return (block_out, attended)


def solution(mesh):
    return jax.shard_map(
        local,
        mesh=mesh,
        in_specs=(P("ta", "ha", "wa", None), P(), P(), P(None, ("ta", "wa"), None, None)),
        out_specs=(P("ta", "ha", "wa", None), P(None, "ha", None, ("ta", "wa"), None)),
        check_vma=False,
    )
```

```python
import functools
import math

import jax
import jax.numpy as jnp
from jax import lax
from jax.experimental import pallas as pl
from jax.experimental.pallas import tpu as pltpu
from jax.sharding import PartitionSpec as P


WIN = 4
NEG = -1e30
LANES = 128


def project_body(place, own, other, w0, w1, w2, w3, out):
    core = place[0]
    rows, cols, depth = own.shape
    cells = jnp.concatenate(
        [own[...].reshape(rows * cols, depth), other[...].reshape(rows * cols, depth)], axis=0
    )
    for d, w_ref in enumerate((w0, w1, w2, w3)):
        wide = 3 * w_ref.shape[2]
        weight = jnp.concatenate([w_ref[0], w_ref[1], w_ref[2]], axis=1)
        got = jnp.dot(cells, weight, preferred_element_type=jnp.float32).astype(jnp.bfloat16)
        got = got.reshape(2, rows, cols, wide)
        lanes = slice(d * wide, (d + 1) * wide)
        out[pl.ds(core * rows, rows), :, lanes] = got[0]
        out[pl.ds((1 - core) * rows, rows), :, lanes] = got[1]


def project(place, own, other, weights):
    rows, cols, depth = own.shape
    wide = 3 * weights[0].shape[2] * len(weights)
    vmem = pl.BlockSpec(memory_space=pltpu.VMEM)
    return pl.pallas_call(
        project_body,
        out_shape=jax.ShapeDtypeStruct((2 * rows, cols, wide), jnp.bfloat16),
        in_specs=[pl.BlockSpec(memory_space=pltpu.SMEM)] + [vmem] * 6,
        out_specs=vmem,
        compiler_params=pltpu.CompilerParams(vmem_limit_bytes=16 * 2**20),
        cost_estimate=pl.CostEstimate(
            flops=4 * rows * cols * depth * wide, bytes_accessed=4 * 2**20, transcendentals=0
        ),
        name="project",
    )(place, own, other, *weights)


def head_body(d, scale, place, bias, p0, p1, p2, p3, out_ref):
    slots = (p0, p1, p2, p3)
    col, flip = place[1], place[2]
    rows, cols, _ = p0.shape
    size = out_ref.shape[3]
    span = WIN * 4 * cols

    def load(at, which):
        lane = (3 * d + which) * size
        return jnp.concatenate(
            [p[at : at + WIN, :, lane : lane + size].reshape(WIN * cols, size) for p in slots],
            axis=0,
        )

    def row_of(dim):
        return (lax.broadcasted_iota(jnp.int32, (span, span), dim) // cols) % WIN

    q_row, k_row = row_of(0), row_of(1)
    above = jnp.where(k_row >= q_row, 0.0, NEG)
    below = jnp.where(k_row <= q_row, 0.0, NEG)
    ones = jnp.ones((span, size), jnp.bfloat16)
    steps = (rows - 2 * WIN) // WIN
    half = steps // 2
    for r in range(steps):
        query = load(WIN + r * WIN, 0)
        parts = []
        for part in range(3):
            score = lax.dot_general(
                query,
                load((r + part) * WIN, 1),
                (((1,), (1,)), ((), ())),
                preferred_element_type=jnp.float32,
            ) * scale
            if part == 0:
                score = score + above
                if r == 0:
                    score = score + bias[0]
            if part == 2:
                score = score + below
                if r == steps - 1:
                    score = score + bias[1]
            parts.append(score)
        peak = jnp.max(jnp.maximum(jnp.maximum(parts[0], parts[1]), parts[2]), axis=1, keepdims=True)
        total = None
        for part in range(3):
            prob = jnp.exp2(parts[part] - peak).astype(jnp.bfloat16)
            value = jnp.concatenate([load((r + part) * WIN, 2), ones], axis=1)
            term = jnp.dot(prob, value, preferred_element_type=jnp.float32)
            total = term if total is None else total + term
        result = (total[:, :size] / total[:, size:]).astype(jnp.bfloat16)
        result = result.reshape(4, WIN, cols, size)
        at = (r % half) * WIN
        for slot in range(4):
            out_ref[(r // half) ^ flip, at : at + WIN, pl.ds((col ^ slot) * cols, cols), :] = result[slot]


def one_head(d, size, place, bias, slots):
    rows, cols, _ = slots[0].shape
    vmem = pl.BlockSpec(memory_space=pltpu.VMEM)
    queries = (rows - 2 * WIN) * 4 * cols
    return pl.pallas_call(
        functools.partial(head_body, d, math.log2(math.e) * size**-0.5),
        out_shape=jax.ShapeDtypeStruct((2, rows // 2 - WIN, 4 * cols, size), jnp.bfloat16),
        in_specs=[pl.BlockSpec(memory_space=pltpu.SMEM)] * 2 + [vmem] * 4,
        out_specs=vmem,
        compiler_params=pltpu.CompilerParams(vmem_limit_bytes=16 * 2**20),
        cost_estimate=pl.CostEstimate(
            flops=6 * queries * 12 * 4 * cols * size,
            bytes_accessed=2**20,
            transcendentals=queries * 12 * 4 * cols,
        ),
        name="head",
    )(place, bias, *slots)


def activated(cells, gain):
    cells = cells.astype(jnp.float32)
    rms = lax.rsqrt(jnp.mean(cells * cells, axis=-1, keepdims=True) + 1e-06)
    scaled = cells * rms * gain
    return scaled / (1.0 + jnp.exp(-scaled))


def conv_body(
    place_ref, own, before, after, rim, rim_before, rim_after, left, right, gain, w_ref,
    block_ref, keep_ref, give_ref, taps, raw, left_n, right_n, sums,
):
    core, frame = place_ref[0], place_ref[2]
    frames, h_dev, w_dev, channels = own.shape
    rim_rows = rim.shape[1]
    far = rim_rows - 1
    rows = h_dev + far - 1
    own_at = jnp.where(core == 0, far, 1)
    far_at = jnp.where(core == 0, 0, h_dev + 1)
    near_at = jnp.where(core == 0, h_dev + far, 0)
    scale = gain[...].reshape(1, 1, channels)

    for side_ref, to in ((left, left_n), (right, right_n)):
        to[...] = activated(side_ref[...], scale)
    col = lax.broadcasted_iota(jnp.int32, (1, w_dev, channels), 1)

    def put(source, lead, t, start, count, at, skip, keep_raw):
        raw_cells = source[lead, start : start + count]
        if keep_raw:
            raw[t - 1, pl.ds(at, count)] = raw_cells
        cells = activated(raw_cells, scale)
        flat = cells.reshape(count * w_dev, channels)
        back = pltpu.roll(flat, 1, 0).reshape(cells.shape)
        ahead = pltpu.roll(flat, count * w_dev - 1, 0).reshape(cells.shape)
        lo = left_n[t, skip : skip + count].reshape(count, 1, channels)
        hi = right_n[t, skip : skip + count].reshape(count, 1, channels)
        to = taps.at[t, pl.ds(at, count)]
        to[:, :, :channels] = jnp.where(col == 0, lo, back).astype(jnp.bfloat16)
        to[:, :, channels : 2 * channels] = cells.astype(jnp.bfloat16)
        to[:, :, 2 * channels :] = jnp.where(col == w_dev - 1, hi, ahead).astype(jnp.bfloat16)

    for t in range(frames + 2):
        if t == 0:
            main, edge, lead = before, rim_before, 0
        elif t == frames + 1:
            main, edge, lead = after, rim_after, 0
        else:
            main, edge, lead = own, rim, t - 1
        inner = 0 < t <= frames
        for start in range(0, h_dev, 8):
            put(main, lead, t, start, 8, own_at + start, start, inner)
        put(edge, lead, t, 0, far, far_at, h_dev, inner)
        put(edge, lead, t, far, 1, near_at, h_dev + far, inner)

    half = rows // 2
    pieces = channels // LANES

    def convolve(t, start):
        parts = [
            taps[t + a, pl.ds(start + b, half)].reshape(half * w_dev, 3 * channels)
            for a in range(3)
            for b in range(3)
        ]
        total = jnp.dot(parts[0], w_ref[0], preferred_element_type=jnp.float32)
        for i in range(1, 9):
            total = total + jnp.dot(parts[i], w_ref[i], preferred_element_type=jnp.float32)
        return total

    for k, out in ((0, keep_ref), (1, give_ref)):
        t = frame ^ k

        def chunk(j, _):
            start = j * half
            total = convolve(t, start)
            base = raw[t, pl.ds(start + 1, half)].astype(jnp.float32)
            total = (total.reshape(half, w_dev, channels) + base).astype(jnp.bfloat16)
            block = total.astype(jnp.float32)
            for piece in range(pieces):
                sums[piece, pl.ds(start, half)] = block[:, :, piece * LANES : (piece + 1) * LANES]
            return 0

        lax.fori_loop(0, 2, chunk, 0)
        for piece in range(pieces):
            lanes = slice(piece * LANES, (piece + 1) * LANES)
            block_ref[t, :, :, lanes] = sums[piece, pl.ds(own_at - 1, h_dev)].astype(jnp.bfloat16)
            for dw in range(2):
                picked = sums[piece, :, pl.ds(dw, w_dev // 2, stride=2), :].astype(jnp.bfloat16)
                picked = picked.reshape(rows // 2, 2, w_dev // 2, LANES)
                for dh in range(2):
                    at = (2 * dh + dw) * channels + piece * LANES
                    out[:, :, at : at + LANES] = picked[:, dh]


def conv_block(place, own, before, after, rim, rim_before, rim_after, left, right, gain, weight):
    frames, h_dev, w_dev, channels = own.shape
    rows = h_dev + rim.shape[1] - 2
    vmem = pl.BlockSpec(memory_space=pltpu.VMEM)
    patch = jax.ShapeDtypeStruct((rows // 2, w_dev // 2, 4 * channels), jnp.bfloat16)
    return pl.pallas_call(
        conv_body,
        out_shape=(jax.ShapeDtypeStruct(own.shape, jnp.bfloat16), patch, patch),
        in_specs=[pl.BlockSpec(memory_space=pltpu.SMEM)] + [vmem] * 10,
        out_specs=(vmem, vmem, vmem),
        scratch_shapes=[
            pltpu.VMEM((frames + 2, rows + 2, w_dev, 3 * channels), jnp.bfloat16),
            pltpu.VMEM((frames, rows + 2, w_dev, channels), jnp.bfloat16),
            pltpu.VMEM(left.shape, jnp.float32),
            pltpu.VMEM(left.shape, jnp.float32),
            pltpu.VMEM((channels // LANES, rows, w_dev, LANES), jnp.float32),
        ],
        compiler_params=pltpu.CompilerParams(vmem_limit_bytes=40 * 2**20),
        cost_estimate=pl.CostEstimate(
            flops=2 * 27 * frames * rows * w_dev * channels * channels,
            bytes_accessed=8 * 2**20,
            transcendentals=2**20,
        ),
        name="conv",
    )(place, own, before, after, rim, rim_before, rim_after, left, right, gain, weight)


def ends(cells, axis, dim, width):
    count = lax.axis_size(axis)
    head = lax.slice_in_dim(cells, 0, width, axis=dim)
    tail = lax.slice_in_dim(cells, cells.shape[dim] - width, cells.shape[dim], axis=dim)
    return (
        lax.ppermute(tail, axis, [(i, i + 1) for i in range(count - 1)]),
        lax.ppermute(head, axis, [(i + 1, i) for i in range(count - 1)]),
    )


def block_and_attention(latents, norm_gain, conv_weight, qkv_weight):
    t_dev, h_dev, w_dev, channels = latents.shape
    n_ta, n_ha, n_wa = lax.axis_size("ta"), lax.axis_size("ha"), lax.axis_size("wa")
    a, h, w = lax.axis_index("ta"), lax.axis_index("ha"), lax.axis_index("wa")
    core, frame = h % 2, w % 2
    reach = 2 * WIN

    def everywhere(to):
        pairs = []
        for ta in range(n_ta):
            for ha in range(n_ha):
                for wa in range(n_wa):
                    dest = to(ta, ha, wa)
                    if dest is not None:
                        ta2, ha2, wa2 = dest
                        pairs.append(
                            ((ta * n_ha + ha) * n_wa + wa, (ta2 * n_ha + ha2) * n_wa + wa2)
                        )
        return pairs

    axes = ("ta", "ha", "wa")
    head, tail = latents[:, : reach + 1], latents[:, h_dev - reach - 1 :]
    first = core == 0
    odd = [(i, i + 1) for i in range(1, n_ha - 1, 2)]
    rim_far = lax.ppermute(jnp.where(first, head, tail), "ha", odd + [(j, i) for i, j in odd])
    before, after = ends(latents, "ta", 0, 1)
    rim_near = lax.ppermute(
        jnp.where(first, tail[:, reach:], head[:, :1]), "ha", [(i, i ^ 1) for i in range(n_ha)]
    )
    rim = jnp.concatenate([rim_far, rim_near], axis=1)
    rim_before, rim_after = ends(rim, "ta", 0, 1)
    last = w_dev - 1

    def side(at):
        return jnp.concatenate(
            [
                jnp.concatenate([x[:, :, at] for x in (before, latents, after)], axis=0),
                jnp.concatenate([x[:, :, at] for x in (rim_before, rim, rim_after)], axis=0),
            ],
            axis=1,
        )

    left = lax.ppermute(side(last), "wa", [(i, i + 1) for i in range(n_wa - 1)])
    right = lax.ppermute(side(0), "wa", [(i + 1, i) for i in range(n_wa - 1)])
    place = jnp.stack([core, w, frame]).astype(jnp.int32)

    mine = qkv_weight[:, 0].transpose(1, 0, 2)
    swapped = lax.ppermute(
        mine,
        axes,
        everywhere(lambda ta, ha, wa: (ta, ha, wa ^ 1) if (wa ^ 1) % 2 != ha % 2 else None),
    )
    mine = jnp.where(core == frame, mine, swapped)
    weights = [mine] + [
        lax.ppermute(mine, "ta", [(i, (i + d) % n_ta) for i in range(n_ta)])
        for d in range(1, n_ta)
    ]

    block_out, keep, give = conv_block(
        place, latents, before, after, rim, rim_before, rim_after, left, right,
        norm_gain[None], conv_weight.reshape(9, 3 * channels, channels),
    )
    own = [keep] + [
        lax.ppermute(give if d % 2 else keep, "wa", [(i, i ^ d) for i in range(n_wa)])
        for d in range(1, n_wa)
    ]
    other = [lax.ppermute(x, "ha", [(j, j ^ 1) for j in range(n_ha)]) for x in own]

    chip = h // 2
    bias = jnp.stack(
        [jnp.where(chip == 0, NEG, 0.0), jnp.where(chip == n_ha // 2 - 1, NEG, 0.0)]
    ).astype(jnp.float32)
    slots = [project(place, own[i], other[i], weights) for i in range(4)]
    result = None
    for d in range(n_ta - 1, -1, -1):
        out = one_head(d, qkv_weight.shape[3], place, bias, slots)
        for kind in range(2):
            moved = lax.ppermute(
                out[kind],
                axes,
                everywhere(
                    lambda ta, ha, wa: (
                        (ta - d) % n_ta,
                        ha - ha % 2 + (wa % 2) ^ kind,
                        wa - wa % 2 + ha % 2,
                    )
                ),
            )
            if result is None:
                result = jnp.zeros((n_ta * t_dev,) + moved.shape, moved.dtype)
            at = (a + d) % n_ta * t_dev + (core ^ kind)
            result = lax.dynamic_update_slice_in_dim(result, moved[None], at, 0)
    return block_out, result[:, :, :, None, :]


def solution(mesh):
    return jax.shard_map(
        block_and_attention,
        mesh=mesh,
        in_specs=(P("ta", "ha", "wa", None), P(), P(), P(None, ("ta", "wa"), None, None)),
        out_specs=(P("ta", "ha", "wa", None), P(None, "ha", None, ("ta", "wa"), None)),
        check_vma=False,
    )
```

```python
import functools
import math

import jax
import jax.numpy as jnp
from jax import lax
from jax.experimental import pallas as pl
from jax.experimental.pallas import tpu as pltpu
from jax.sharding import PartitionSpec as P


WIN = 4
NEG = -1e30
LANES = 128


def where():
    a, h, w = lax.axis_index("ta"), lax.axis_index("ha"), lax.axis_index("wa")
    top = jnp.where(h < 2, 1, 0)
    bottom = jnp.where(h >= lax.axis_size("ha") - 2, 1, 0)
    return lax.rem(h, 2), w, lax.rem(w, 2), top, bottom, a


def faces_body(cells, far, near, first, last, sems):
    core = where()[0]
    end = cells.shape[1] - 1
    far_at = core * end
    moves = [(cells.at[0], first), (cells.at[1], last)]
    for t in range(2):
        moves += [(cells.at[t, far_at], far.at[t]), (cells.at[t, end - far_at], near.at[t])]
    copies = [pltpu.make_async_copy(x, y, sems.at[i]) for i, (x, y) in enumerate(moves)]
    for copy in copies:
        copy.start()
    for copy in copies:
        copy.wait()


def faces(cells):
    _, rows, cols, depth = cells.shape
    vmem = pl.BlockSpec(memory_space=pltpu.VMEM)
    row = jax.ShapeDtypeStruct((2, cols, depth), cells.dtype)
    face = jax.ShapeDtypeStruct((rows, cols, depth), cells.dtype)
    return pl.pallas_call(
        faces_body,
        out_shape=(row, row, face, face),
        in_specs=[pl.BlockSpec(memory_space=pltpu.HBM)],
        out_specs=(vmem,) * 4,
        scratch_shapes=[pltpu.SemaphoreType.DMA((6,))],
        compiler_params=pltpu.CompilerParams(vmem_limit_bytes=4 * 2**20),
        name="faces",
    )(cells)


def project_body(groups, *refs):
    place = where()
    outs = refs[-len(groups) :]
    weights = refs[-len(groups) - 4 : -len(groups)]
    core = place[0]
    sides, at = [], 0
    for first, count in groups:
        own, other = refs[at : at + count], refs[at + count : at + 2 * count]
        at += 2 * count
        rows, cols, depth = own[0].shape
        flat = [ref[...].reshape(rows * cols, depth) for ref in (*own, *other)]
        sides.append((jnp.concatenate(flat, axis=0), count, rows, cols))
    for d, w_ref in enumerate(weights):
        weight = jnp.concatenate([w_ref[i] for i in range(3)], axis=1)
        for (first, _), (cells, count, rows, cols), out in zip(groups, sides, outs):
            size = w_ref.shape[2]
            wide = (3 - first) * size
            got = jnp.dot(
                cells, weight[:, first * size :], preferred_element_type=jnp.float32
            ).astype(jnp.bfloat16)
            got = got.reshape(2, count, rows, cols, wide)
            lanes = slice(d * wide, (d + 1) * wide)
            for i in range(count):
                out[i, pl.ds(core * rows, rows), :, lanes] = got[0, i]
                out[i, pl.ds((1 - core) * rows, rows), :, lanes] = got[1, i]


def project(groups, weights):
    vmem = pl.BlockSpec(memory_space=pltpu.VMEM)
    shapes, cells, flops = [], [], 0
    for first, own, other in groups:
        rows, cols, depth = own[0].shape
        wide = (3 - first) * weights[0].shape[2] * len(weights)
        shapes.append(jax.ShapeDtypeStruct((len(own), 2 * rows, cols, wide), jnp.bfloat16))
        cells += [*own, *other]
        flops += 4 * len(own) * rows * cols * depth * wide
    return pl.pallas_call(
        functools.partial(project_body, [(first, len(own)) for first, own, _ in groups]),
        out_shape=tuple(shapes),
        in_specs=[vmem] * (len(cells) + 4),
        out_specs=(vmem,) * len(shapes),
        compiler_params=pltpu.CompilerParams(vmem_limit_bytes=12 * 2**20),
        cost_estimate=pl.CostEstimate(flops=flops, bytes_accessed=4 * 2**20, transcendentals=0),
        name="project",
    )(*cells, *weights)


def attend(scale, steps, r, place, load):
    size = load(1, 0).shape[1]
    span = load(1, 0).shape[0]
    cols = span // (4 * WIN)

    def row_of(dim):
        return (lax.broadcasted_iota(jnp.int32, (span, span), dim) // cols) % WIN

    query = load(r + 1, 0)
    parts = []
    for part in range(3):
        score = lax.dot_general(
            query,
            load(r + part, 1),
            (((1,), (1,)), ((), ())),
            preferred_element_type=jnp.float32,
        ) * scale
        if part == 0:
            score = score + jnp.where(row_of(1) >= row_of(0), 0.0, NEG)
            if r == 0:
                score = score + jnp.where(place[3] == 1, NEG, 0.0)
        if part == 2:
            score = score + jnp.where(row_of(1) <= row_of(0), 0.0, NEG)
            if r == steps - 1:
                score = score + jnp.where(place[4] == 1, NEG, 0.0)
        parts.append(score)
    peak = jnp.max(jnp.maximum(jnp.maximum(parts[0], parts[1]), parts[2]), axis=1, keepdims=True)
    total = None
    ones = jnp.ones((span, size), jnp.bfloat16)
    for part in range(3):
        prob = jnp.exp2(parts[part] - peak).astype(jnp.bfloat16)
        value = jnp.concatenate([load(r + part, 2), ones], axis=1)
        term = jnp.dot(prob, value, preferred_element_type=jnp.float32)
        total = term if total is None else total + term
    result = (total[:, :size] / total[:, size:]).astype(jnp.bfloat16)
    return result.reshape(4, WIN, cols, size)


def loader(d, size, slots, halo):
    _, rows, cols, _ = slots[0].shape
    groups = rows // WIN + 2

    def load(group, which):
        if 0 < group < groups - 1:
            at, lane = (group - 1) * WIN, (3 * d + which) * size
            parts = [p[0, at : at + WIN, :, lane : lane + size] for p in slots]
        else:
            at, lane = min(group, 1) * WIN, (2 * d + which - 1) * size
            parts = [halo[i, at : at + WIN, :, lane : lane + size] for i in range(4)]
        return jnp.concatenate([x.reshape(WIN * cols, size) for x in parts], axis=0)

    return load


def inner_body(scale, p0, p1, p2, p3, out_ref):
    place = where()
    slots = (p0, p1, p2, p3)
    heads, count, _, _, size = out_ref.shape
    cols = p0.shape[2]
    for d in range(heads):
        load = loader(d, size, slots, None)
        for i in range(count):
            result = attend(scale, count + 2, i + 1, place, load)
            for slot in range(4):
                out_ref[d, i, :, pl.ds((place[1] ^ slot) * cols, cols), :] = result[slot]


def outer_body(d, scale, p0, p1, p2, p3, halo, inner, out_ref):
    place = where()
    slots = (p0, p1, p2, p3)
    size = out_ref.shape[3]
    cols = p0.shape[2]
    load = loader(d, size, slots, halo)
    flip = place[2]
    steps = inner.shape[1] + 2
    half = steps // 2
    for r in range(steps):
        band, at = (r // half) ^ flip, (r % half) * WIN
        if 0 < r < steps - 1:
            out_ref[band, at : at + WIN] = inner[d, r - 1]
            continue
        result = attend(scale, steps, r, place, load)
        for slot in range(4):
            out_ref[band, at : at + WIN, pl.ds((place[1] ^ slot) * cols, cols), :] = result[slot]


def cost(queries, cols, size):
    keys = 12 * 4 * cols
    return pl.CostEstimate(
        flops=6 * queries * keys * size, bytes_accessed=2**20, transcendentals=queries * keys
    )


def inner_heads(heads, size, slots):
    _, rows, cols, _ = slots[0].shape
    count = rows // WIN - 2
    vmem = pl.BlockSpec(memory_space=pltpu.VMEM)
    return pl.pallas_call(
        functools.partial(inner_body, math.log2(math.e) * size**-0.5),
        out_shape=jax.ShapeDtypeStruct((heads, count, WIN, 4 * cols, size), jnp.bfloat16),
        in_specs=[vmem] * 4,
        out_specs=vmem,
        compiler_params=pltpu.CompilerParams(vmem_limit_bytes=12 * 2**20),
        cost_estimate=cost(heads * count * WIN * 4 * cols, cols, size),
        name="inner",
    )(*slots)


def one_head(d, size, slots, halo, inner):
    _, rows, cols, _ = slots[0].shape
    vmem = pl.BlockSpec(memory_space=pltpu.VMEM)
    return pl.pallas_call(
        functools.partial(outer_body, d, math.log2(math.e) * size**-0.5),
        out_shape=jax.ShapeDtypeStruct((2, rows // 2, 4 * cols, size), jnp.bfloat16),
        in_specs=[vmem] * 6,
        out_specs=vmem,
        compiler_params=pltpu.CompilerParams(vmem_limit_bytes=12 * 2**20),
        cost_estimate=cost(2 * WIN * 4 * cols, cols, size),
        name="head",
    )(*slots, halo, inner)


def activated(cells, gain):
    cells = cells.astype(jnp.float32)
    rms = lax.rsqrt(jnp.mean(cells * cells, axis=-1, keepdims=True) + 1e-06)
    scaled = cells * rms * gain
    return scaled / (1.0 + jnp.exp(-scaled))


def conv_body(
    own, before, after, rim, rim_before, rim_after, left, right, gain, w_ref,
    block_ref, keep_ref, give_ref, edge_ref, taps, raw, left_n, right_n, sums,
):
    core, frame = where()[0], where()[2]
    frames, h_dev, w_dev, channels = own.shape
    rim_rows = rim.shape[1]
    far = rim_rows - 1
    rows = h_dev + far - 1
    own_at = jnp.where(core == 0, far, 1)
    far_at = jnp.where(core == 0, 0, h_dev + 1)
    near_at = jnp.where(core == 0, h_dev + far, 0)
    scale = gain[...].reshape(1, 1, channels)

    for side_ref, to in ((left, left_n), (right, right_n)):
        to[...] = activated(side_ref[...], scale)
    col = lax.broadcasted_iota(jnp.int32, (1, w_dev, channels), 1)

    def put(source, lead, t, start, count, at, skip, keep_raw):
        raw_cells = source[lead, start : start + count]
        if keep_raw:
            raw[t - 1, pl.ds(at, count)] = raw_cells
        cells = activated(raw_cells, scale)
        flat = cells.reshape(count * w_dev, channels)
        back = pltpu.roll(flat, 1, 0).reshape(cells.shape)
        ahead = pltpu.roll(flat, count * w_dev - 1, 0).reshape(cells.shape)
        lo = left_n[t, skip : skip + count].reshape(count, 1, channels)
        hi = right_n[t, skip : skip + count].reshape(count, 1, channels)
        to = taps.at[t, pl.ds(at, count)]
        to[:, :, :channels] = jnp.where(col == 0, lo, back).astype(jnp.bfloat16)
        to[:, :, channels : 2 * channels] = cells.astype(jnp.bfloat16)
        to[:, :, 2 * channels :] = jnp.where(col == w_dev - 1, hi, ahead).astype(jnp.bfloat16)

    for t in range(frames + 2):
        if t == 0:
            main, edge, lead = before, rim_before, 0
        elif t == frames + 1:
            main, edge, lead = after, rim_after, 0
        else:
            main, edge, lead = own, rim, t - 1
        inner = 0 < t <= frames
        for start in range(0, h_dev, 8):
            put(main, lead, t, start, 8, own_at + start, start, inner)
        put(edge, lead, t, 0, far, far_at, h_dev, inner)
        put(edge, lead, t, far, 1, near_at, h_dev + far, inner)

    chunk_rows = rows
    pieces = channels // LANES

    def convolve(t, start):
        parts = [
            taps[t + a, pl.ds(start + b, chunk_rows)].reshape(chunk_rows * w_dev, 3 * channels)
            for a in range(3)
            for b in range(3)
        ]
        total = jnp.dot(parts[0], w_ref[0], preferred_element_type=jnp.float32)
        for i in range(1, 9):
            total = total + jnp.dot(parts[i], w_ref[i], preferred_element_type=jnp.float32)
        return total

    for k, out in ((0, keep_ref), (1, give_ref)):
        t = frame ^ k

        def chunk(j, _):
            start = j * chunk_rows
            total = convolve(t, start)
            base = raw[t, pl.ds(start + 1, chunk_rows)].astype(jnp.float32)
            total = (total.reshape(chunk_rows, w_dev, channels) + base).astype(jnp.bfloat16)
            block = total.astype(jnp.float32)
            for piece in range(pieces):
                sums[piece, pl.ds(start, chunk_rows)] = block[:, :, piece * LANES : (piece + 1) * LANES]
            return 0

        lax.fori_loop(0, rows // chunk_rows, chunk, 0)
        for piece in range(pieces):
            lanes = slice(piece * LANES, (piece + 1) * LANES)
            block_ref[t, :, :, lanes] = sums[piece, pl.ds(own_at - 1, h_dev)].astype(jnp.bfloat16)
            for dw in range(2):
                picked = sums[piece, :, pl.ds(dw, w_dev // 2, stride=2), :].astype(jnp.bfloat16)
                picked = picked.reshape(rows // 2, 2, w_dev // 2, LANES)
                for dh in range(2):
                    at = (2 * dh + dw) * channels + piece * LANES
                    out[:, :, at : at + LANES] = picked[:, dh]
        edge_ref[k] = out[pl.ds(core * (rows // 2 - WIN), WIN)]


def conv_block(own, before, after, rim, rim_before, rim_after, left, right, gain, weight):
    frames, h_dev, w_dev, channels = own.shape
    rows = h_dev + rim.shape[1] - 2
    vmem = pl.BlockSpec(memory_space=pltpu.VMEM)
    patch = jax.ShapeDtypeStruct((rows // 2, w_dev // 2, 4 * channels), jnp.bfloat16)
    edge = jax.ShapeDtypeStruct((2, WIN, w_dev // 2, 4 * channels), jnp.bfloat16)
    return pl.pallas_call(
        conv_body,
        out_shape=(jax.ShapeDtypeStruct(own.shape, jnp.bfloat16), patch, patch, edge),
        in_specs=[vmem] * 10,
        out_specs=(vmem,) * 4,
        scratch_shapes=[
            pltpu.VMEM((frames + 2, rows + 2, w_dev, 3 * channels), jnp.bfloat16),
            pltpu.VMEM((frames, rows + 2, w_dev, channels), jnp.bfloat16),
            pltpu.VMEM(left.shape, jnp.float32),
            pltpu.VMEM(left.shape, jnp.float32),
            pltpu.VMEM((channels // LANES, rows, w_dev, LANES), jnp.float32),
        ],
        compiler_params=pltpu.CompilerParams(vmem_limit_bytes=20 * 2**20),
        cost_estimate=pl.CostEstimate(
            flops=2 * 27 * frames * rows * w_dev * channels * channels,
            bytes_accessed=8 * 2**20,
            transcendentals=2**20,
        ),
        name="conv",
    )(own, before, after, rim, rim_before, rim_after, left, right, gain, weight)


def permute(cells, axis, pairs):
    if cells.shape[-2] % 16:
        return lax.ppermute(cells, axis, pairs)
    flat = cells.reshape(-1, cells.shape[-1])
    return lax.ppermute(flat, axis, pairs).reshape(cells.shape)


def ends(cells, axis, dim, width):
    count = lax.axis_size(axis)
    head = lax.slice_in_dim(cells, 0, width, axis=dim)
    tail = lax.slice_in_dim(cells, cells.shape[dim] - width, cells.shape[dim], axis=dim)
    return (
        permute(tail, axis, [(i, i + 1) for i in range(count - 1)]),
        permute(head, axis, [(i + 1, i) for i in range(count - 1)]),
    )


def choose_body(mine, swapped, out):
    place = where()

    @pl.when(place[0] == place[2])
    def _():
        out[...] = mine[...]

    @pl.when(place[0] != place[2])
    def _():
        out[...] = swapped[...]


def choose(mine, swapped):
    vmem = pl.BlockSpec(memory_space=pltpu.VMEM)
    return pl.pallas_call(
        choose_body,
        out_shape=jax.ShapeDtypeStruct(mine.shape, mine.dtype),
        in_specs=[vmem, vmem],
        out_specs=vmem,
        compiler_params=pltpu.CompilerParams(vmem_limit_bytes=4 * 2**20),
        name="choose",
    )(mine, swapped)


def assemble_body(count, order, *refs):
    place = where()
    pieces, out, sems = refs[: 2 * len(order)], refs[-2], refs[-1]
    copies = []
    for i, d in enumerate(order):
        for kind in range(2):
            at = (place[5] + d) % count * 2 + (place[0] ^ kind)
            n = 2 * i + kind
            copies.append(pltpu.make_async_copy(pieces[n], out.at[at], sems.at[n]))
            copies[-1].start()
    for copy in copies:
        copy.wait()


def assemble(count, order, pieces):
    vmem = pl.BlockSpec(memory_space=pltpu.VMEM)
    return pl.pallas_call(
        functools.partial(assemble_body, count, order),
        out_shape=jax.ShapeDtypeStruct((len(pieces),) + pieces[0].shape, jnp.bfloat16),
        in_specs=[vmem] * len(pieces),
        out_specs=pl.BlockSpec(memory_space=pl.ANY),
        scratch_shapes=[pltpu.SemaphoreType.DMA((len(pieces),))],
        compiler_params=pltpu.CompilerParams(vmem_limit_bytes=4 * 2**20),
        name="assemble",
    )(*pieces)


def block_and_attention(latents, norm_gain, conv_weight, qkv_weight):
    _, _, w_dev, channels = latents.shape
    n_ta, n_ha, n_wa = lax.axis_size("ta"), lax.axis_size("ha"), lax.axis_size("wa")

    def everywhere(to):
        pairs = []
        for ta in range(n_ta):
            for ha in range(n_ha):
                for wa in range(n_wa):
                    dest = to(ta, ha, wa)
                    if dest is not None:
                        ta2, ha2, wa2 = dest
                        pairs.append(
                            ((ta * n_ha + ha) * n_wa + wa, (ta2 * n_ha + ha2) * n_wa + wa2)
                        )
        return pairs

    axes = ("ta", "ha", "wa")
    far_row, near_row, first, last = faces(latents)
    odd = [(i, i + 1) for i in range(1, n_ha - 1, 2)]
    odd += [(j, i) for i, j in odd]
    rim_far = permute(far_row[:, None], "ha", odd)
    ups = [(i, i + 1) for i in range(n_ta - 1)]
    before = permute(last[None], "ta", ups)
    after = permute(first[None], "ta", [(j, i) for i, j in ups])
    rim_near = permute(near_row[:, None], "ha", [(i, i ^ 1) for i in range(n_ha)])
    rim = jnp.concatenate([rim_far, rim_near], axis=1)
    rim_before, rim_after = ends(rim, "ta", 0, 1)
    last = w_dev - 1

    def side(at):
        return jnp.concatenate(
            [
                jnp.concatenate([x[:, :, at] for x in (before, latents, after)], axis=0),
                jnp.concatenate([x[:, :, at] for x in (rim_before, rim, rim_after)], axis=0),
            ],
            axis=1,
        )

    left = permute(side(last), "wa", [(i, i + 1) for i in range(n_wa - 1)])
    right = permute(side(0), "wa", [(i + 1, i) for i in range(n_wa - 1)])
    mine = qkv_weight[:, 0].transpose(1, 0, 2)
    swapped = permute(
        mine,
        axes,
        everywhere(lambda ta, ha, wa: (ta, ha, wa ^ 1) if (wa ^ 1) % 2 != ha % 2 else None),
    )
    mine = choose(mine, swapped)
    weights = [mine] + [
        permute(mine, "ta", [(i, (i + d) % n_ta) for i in range(n_ta)])
        for d in range(1, n_ta)
    ]

    block_out, keep, give, edge = conv_block(
        latents, before, after, rim, rim_before, rim_after, left, right,
        norm_gain[None], conv_weight.reshape(9, 3 * channels, channels),
    )
    own = [keep] + [
        permute(give if d % 2 else keep, "wa", [(i, i ^ d) for i in range(n_wa)])
        for d in range(1, n_wa)
    ]
    other = [permute(x, "ha", [(j, j ^ 1) for j in range(n_ha)]) for x in own]

    edge = permute(edge, "ha", odd)
    rows_own = [edge[0]] + [
        permute(edge[d % 2], "wa", [(i, i ^ d) for i in range(n_wa)])
        for d in range(1, n_wa)
    ]
    rows_other = [permute(x, "ha", [(j, j ^ 1) for j in range(n_ha)]) for x in rows_own]
    slots = [project([(0, [own[i]], [other[i]])], weights)[0] for i in range(4)]
    heads, size = n_ta, qkv_weight.shape[3]
    inner = inner_heads(heads, size, slots)
    (halo,) = project([(1, rows_own, rows_other)], weights)
    pieces = []
    for d in range(heads - 1, -1, -1):
        out = one_head(d, size, slots, halo, inner)
        moved = permute(
            out,
            axes,
            everywhere(
                lambda ta, ha, wa: (
                    (ta - d) % n_ta,
                    ha - ha % 2 + wa % 2,
                    wa - wa % 2 + ha % 2,
                )
            ),
        )
        crossed = permute(moved[1], "ha", [(j, j ^ 1) for j in range(n_ha)])
        pieces += [moved[0], crossed]
    result = assemble(n_ta, list(range(heads - 1, -1, -1)), pieces)
    return block_out, result[:, :, :, None, :]


def solution(mesh):
    return jax.shard_map(
        block_and_attention,
        mesh=mesh,
        in_specs=(P("ta", "ha", "wa", None), P(), P(), P(None, ("ta", "wa"), None, None)),
        out_specs=(P("ta", "ha", "wa", None), P(None, "ha", None, ("ta", "wa"), None)),
        check_vma=False,
    )
```

```python
import functools
import math

import jax
import jax.numpy as jnp
from jax import lax
from jax.experimental import pallas as pl
from jax.experimental.pallas import tpu as pltpu
from jax.sharding import PartitionSpec as P


WIN = 4
NEG = -1e30
LANES = 128


def where():
    a, h, w = lax.axis_index("ta"), lax.axis_index("ha"), lax.axis_index("wa")
    top = jnp.where(h < 2, 1, 0)
    bottom = jnp.where(h >= lax.axis_size("ha") - 2, 1, 0)
    return lax.rem(h, 2), w, lax.rem(w, 2), top, bottom, a


def faces_body(cells, gain, far, near, first, last, gain_out, sems):
    gain_out[...] = gain[...]
    core = where()[0]
    end = cells.shape[1] - 1
    far_at = core * end
    moves = [(cells.at[0], first), (cells.at[1], last)]
    for t in range(2):
        moves += [(cells.at[t, far_at], far.at[t]), (cells.at[t, end - far_at], near.at[t])]
    copies = [pltpu.make_async_copy(x, y, sems.at[i]) for i, (x, y) in enumerate(moves)]
    for copy in copies:
        copy.start()
    for copy in copies:
        copy.wait()


def faces(cells, gain):
    _, rows, cols, depth = cells.shape
    vmem = pl.BlockSpec(memory_space=pltpu.VMEM)
    row = jax.ShapeDtypeStruct((2, cols, depth), cells.dtype)
    face = jax.ShapeDtypeStruct((rows, cols, depth), cells.dtype)
    return pl.pallas_call(
        faces_body,
        out_shape=(row, row, face, face, jax.ShapeDtypeStruct(gain.shape, gain.dtype)),
        in_specs=[pl.BlockSpec(memory_space=pltpu.HBM), vmem],
        out_specs=(vmem,) * 5,
        scratch_shapes=[pltpu.SemaphoreType.DMA((6,))],
        compiler_params=pltpu.CompilerParams(vmem_limit_bytes=4 * 2**20),
        name="faces",
    )(cells, gain)


def project_body(groups, *refs):
    place = where()
    outs = refs[-len(groups) :]
    weights = refs[-len(groups) - 4 : -len(groups)]
    core = place[0]
    sides, at = [], 0
    for first, count in groups:
        own, other = refs[at : at + count], refs[at + count : at + 2 * count]
        at += 2 * count
        rows, cols, depth = own[0].shape
        flat = [ref[...].reshape(rows * cols, depth) for ref in (*own, *other)]
        sides.append((jnp.concatenate(flat, axis=0), count, rows, cols))
    for d, w_ref in enumerate(weights):
        weight = jnp.concatenate([w_ref[i] for i in range(3)], axis=1)
        for (first, _), (cells, count, rows, cols), out in zip(groups, sides, outs):
            size = w_ref.shape[2]
            wide = (3 - first) * size
            got = jnp.dot(
                cells, weight[:, first * size :], preferred_element_type=jnp.float32
            ).astype(jnp.bfloat16)
            got = got.reshape(2, count, rows, cols, wide)
            lanes = slice(d * wide, (d + 1) * wide)
            for i in range(count):
                out[i, pl.ds(core * rows, rows), :, lanes] = got[0, i]
                out[i, pl.ds((1 - core) * rows, rows), :, lanes] = got[1, i]


def project(groups, weights):
    vmem = pl.BlockSpec(memory_space=pltpu.VMEM)
    shapes, cells, flops = [], [], 0
    for first, own, other in groups:
        rows, cols, depth = own[0].shape
        wide = (3 - first) * weights[0].shape[2] * len(weights)
        shapes.append(jax.ShapeDtypeStruct((len(own), 2 * rows, cols, wide), jnp.bfloat16))
        cells += [*own, *other]
        flops += 4 * len(own) * rows * cols * depth * wide
    return pl.pallas_call(
        functools.partial(project_body, [(first, len(own)) for first, own, _ in groups]),
        out_shape=tuple(shapes),
        in_specs=[vmem] * (len(cells) + 4),
        out_specs=(vmem,) * len(shapes),
        compiler_params=pltpu.CompilerParams(vmem_limit_bytes=12 * 2**20),
        cost_estimate=pl.CostEstimate(flops=flops, bytes_accessed=4 * 2**20, transcendentals=0),
        name="project",
    )(*cells, *weights)


def attend(scale, steps, r, place, load):
    size = load(1, 0).shape[1]
    span = load(1, 0).shape[0]
    cols = span // (4 * WIN)

    def row_of(dim):
        return (lax.broadcasted_iota(jnp.int32, (span, span), dim) // cols) % WIN

    query = load(r + 1, 0)
    parts = []
    for part in range(3):
        score = lax.dot_general(
            query,
            load(r + part, 1),
            (((1,), (1,)), ((), ())),
            preferred_element_type=jnp.float32,
        ) * scale
        if part == 0:
            score = score + jnp.where(row_of(1) >= row_of(0), 0.0, NEG)
            if r == 0:
                score = score + jnp.where(place[3] == 1, NEG, 0.0)
        if part == 2:
            score = score + jnp.where(row_of(1) <= row_of(0), 0.0, NEG)
            if r == steps - 1:
                score = score + jnp.where(place[4] == 1, NEG, 0.0)
        parts.append(score)
    peak = jnp.max(jnp.maximum(jnp.maximum(parts[0], parts[1]), parts[2]), axis=1, keepdims=True)
    total = None
    ones = jnp.ones((span, size), jnp.bfloat16)
    for part in range(3):
        prob = jnp.exp2(parts[part] - peak).astype(jnp.bfloat16)
        value = jnp.concatenate([load(r + part, 2), ones], axis=1)
        term = jnp.dot(prob, value, preferred_element_type=jnp.float32)
        total = term if total is None else total + term
    result = (total[:, :size] / total[:, size:]).astype(jnp.bfloat16)
    return result.reshape(4, WIN, cols, size)


def loader(d, size, slots, halo):
    _, rows, cols, _ = slots[0].shape
    groups = rows // WIN + 2

    def load(group, which):
        if 0 < group < groups - 1:
            at, lane = (group - 1) * WIN, (3 * d + which) * size
            parts = [p[0, at : at + WIN, :, lane : lane + size] for p in slots]
        else:
            at, lane = min(group, 1) * WIN, (2 * d + which - 1) * size
            parts = [halo[i, at : at + WIN, :, lane : lane + size] for i in range(4)]
        return jnp.concatenate([x.reshape(WIN * cols, size) for x in parts], axis=0)

    return load


def inner_body(scale, p0, p1, p2, p3, out_ref):
    place = where()
    slots = (p0, p1, p2, p3)
    heads, count, _, _, size = out_ref.shape
    cols = p0.shape[2]
    for d in range(heads):
        load = loader(d, size, slots, None)
        for i in range(count):
            result = attend(scale, count + 2, i + 1, place, load)
            for slot in range(4):
                out_ref[d, i, :, pl.ds((place[1] ^ slot) * cols, cols), :] = result[slot]


def outer_body(d, scale, p0, p1, p2, p3, halo, inner, out_ref):
    place = where()
    slots = (p0, p1, p2, p3)
    size = out_ref.shape[3]
    cols = p0.shape[2]
    load = loader(d, size, slots, halo)
    flip = place[2]
    steps = inner.shape[1] + 2
    half = steps // 2
    for r in range(steps):
        band, at = (r // half) ^ flip, (r % half) * WIN
        if 0 < r < steps - 1:
            out_ref[band, at : at + WIN] = inner[d, r - 1]
            continue
        result = attend(scale, steps, r, place, load)
        for slot in range(4):
            out_ref[band, at : at + WIN, pl.ds((place[1] ^ slot) * cols, cols), :] = result[slot]


def cost(queries, cols, size):
    keys = 12 * 4 * cols
    return pl.CostEstimate(
        flops=6 * queries * keys * size, bytes_accessed=2**20, transcendentals=queries * keys
    )


def inner_heads(heads, size, slots):
    _, rows, cols, _ = slots[0].shape
    count = rows // WIN - 2
    vmem = pl.BlockSpec(memory_space=pltpu.VMEM)
    return pl.pallas_call(
        functools.partial(inner_body, math.log2(math.e) * size**-0.5),
        out_shape=jax.ShapeDtypeStruct((heads, count, WIN, 4 * cols, size), jnp.bfloat16),
        in_specs=[vmem] * 4,
        out_specs=vmem,
        compiler_params=pltpu.CompilerParams(vmem_limit_bytes=12 * 2**20),
        cost_estimate=cost(heads * count * WIN * 4 * cols, cols, size),
        name="inner",
    )(*slots)


def one_head(d, size, slots, halo, inner):
    _, rows, cols, _ = slots[0].shape
    vmem = pl.BlockSpec(memory_space=pltpu.VMEM)
    return pl.pallas_call(
        functools.partial(outer_body, d, math.log2(math.e) * size**-0.5),
        out_shape=jax.ShapeDtypeStruct((2, rows // 2, 4 * cols, size), jnp.bfloat16),
        in_specs=[vmem] * 6,
        out_specs=vmem,
        compiler_params=pltpu.CompilerParams(vmem_limit_bytes=12 * 2**20),
        cost_estimate=cost(2 * WIN * 4 * cols, cols, size),
        name="head",
    )(*slots, halo, inner)


def activated(cells, gain):
    cells = cells.astype(jnp.float32)
    rms = lax.rsqrt(jnp.mean(cells * cells, axis=-1, keepdims=True) + 1e-06)
    scaled = cells * rms * gain
    return scaled / (1.0 + jnp.exp(-scaled))


def conv_body(
    own0, own1, before, after, rim, rim_before, rim_after, left, right, gain, w_hbm,
    block_ref, keep_ref, give_ref, edge_ref, taps, raw, left_n, right_n, sums,
    w_ref, w_sem,
):
    fetch = pltpu.make_async_copy(w_hbm, w_ref, w_sem)
    fetch.start()
    core, frame = where()[0], where()[2]
    frames, h_dev, w_dev, channels = (2,) + own0.shape[1:]
    rim_rows = rim.shape[1]
    far = rim_rows - 1
    rows = h_dev + far - 1
    own_at = jnp.where(core == 0, far, 1)
    far_at = jnp.where(core == 0, 0, h_dev + 1)
    near_at = jnp.where(core == 0, h_dev + far, 0)
    scale = gain[...].reshape(1, 1, channels)

    for side_ref, to in ((left, left_n), (right, right_n)):
        to[...] = activated(side_ref[...], scale)
    col = lax.broadcasted_iota(jnp.int32, (1, w_dev, channels), 1)

    def put(source, lead, t, start, count, at, skip, keep_raw):
        raw_cells = source[lead, start : start + count]
        if keep_raw:
            raw[t - 1, pl.ds(at, count)] = raw_cells
        cells = activated(raw_cells, scale)
        flat = cells.reshape(count * w_dev, channels)
        back = pltpu.roll(flat, 1, 0).reshape(cells.shape)
        ahead = pltpu.roll(flat, count * w_dev - 1, 0).reshape(cells.shape)
        lo = left_n[t, skip : skip + count].reshape(count, 1, channels)
        hi = right_n[t, skip : skip + count].reshape(count, 1, channels)
        to = taps.at[t, pl.ds(at, count)]
        to[:, :, :channels] = jnp.where(col == 0, lo, back).astype(jnp.bfloat16)
        to[:, :, channels : 2 * channels] = cells.astype(jnp.bfloat16)
        to[:, :, 2 * channels :] = jnp.where(col == w_dev - 1, hi, ahead).astype(jnp.bfloat16)

    for t in range(frames + 2):
        if t == 0:
            main, edge, lead = before, rim_before, 0
        elif t == frames + 1:
            main, edge, lead = after, rim_after, 0
        else:
            main, edge, lead = (own0, own1)[t - 1], rim, t - 1
        inner = 0 < t <= frames
        for start in range(0, h_dev, 8):
            put(main, 0, t, start, 8, own_at + start, start, inner)
        put(edge, lead, t, 0, far, far_at, h_dev, inner)
        put(edge, lead, t, far, 1, near_at, h_dev + far, inner)

    chunk_rows = rows
    pieces = channels // LANES

    fetch.wait()

    def convolve(t, start):
        parts = [
            taps[t + a, pl.ds(start + b, chunk_rows)].reshape(chunk_rows * w_dev, 3 * channels)
            for a in range(3)
            for b in range(3)
        ]
        total = jnp.dot(parts[0], w_ref[0], preferred_element_type=jnp.float32)
        for i in range(1, 9):
            total = total + jnp.dot(parts[i], w_ref[i], preferred_element_type=jnp.float32)
        return total

    for k, out in ((0, keep_ref), (1, give_ref)):
        t = frame ^ k

        def chunk(j, _):
            start = j * chunk_rows
            total = convolve(t, start)
            base = raw[t, pl.ds(start + 1, chunk_rows)].astype(jnp.float32)
            total = (total.reshape(chunk_rows, w_dev, channels) + base).astype(jnp.bfloat16)
            block = total.astype(jnp.float32)
            for piece in range(pieces):
                sums[piece, pl.ds(start, chunk_rows)] = block[:, :, piece * LANES : (piece + 1) * LANES]
            return 0

        lax.fori_loop(0, rows // chunk_rows, chunk, 0)
        for piece in range(pieces):
            lanes = slice(piece * LANES, (piece + 1) * LANES)
            block_ref[t, :, :, lanes] = sums[piece, pl.ds(own_at - 1, h_dev)].astype(jnp.bfloat16)
            for dw in range(2):
                picked = sums[piece, :, pl.ds(dw, w_dev // 2, stride=2), :].astype(jnp.bfloat16)
                picked = picked.reshape(rows // 2, 2, w_dev // 2, LANES)
                for dh in range(2):
                    at = (2 * dh + dw) * channels + piece * LANES
                    out[:, :, at : at + LANES] = picked[:, dh]
        edge_ref[k] = out[pl.ds(core * (rows // 2 - WIN), WIN)]


def conv_block(own0, own1, before, after, rim, rim_before, rim_after, left, right, gain, weight):
    frames, h_dev, w_dev, channels = (2,) + own0.shape[1:]
    rows = h_dev + rim.shape[1] - 2
    vmem = pl.BlockSpec(memory_space=pltpu.VMEM)
    patch = jax.ShapeDtypeStruct((rows // 2, w_dev // 2, 4 * channels), jnp.bfloat16)
    edge = jax.ShapeDtypeStruct((2, WIN, w_dev // 2, 4 * channels), jnp.bfloat16)
    return pl.pallas_call(
        conv_body,
        out_shape=(jax.ShapeDtypeStruct((2,) + own0.shape[1:], jnp.bfloat16), patch, patch, edge),
        in_specs=[vmem] * 10 + [pl.BlockSpec(memory_space=pltpu.HBM)],
        out_specs=(vmem,) * 4,
        scratch_shapes=[
            pltpu.VMEM((frames + 2, rows + 2, w_dev, 3 * channels), jnp.bfloat16),
            pltpu.VMEM((frames, rows + 2, w_dev, channels), jnp.bfloat16),
            pltpu.VMEM(left.shape, jnp.float32),
            pltpu.VMEM(left.shape, jnp.float32),
            pltpu.VMEM((channels // LANES, rows, w_dev, LANES), jnp.float32),
            pltpu.VMEM(weight.shape, weight.dtype),
            pltpu.SemaphoreType.DMA,
        ],
        compiler_params=pltpu.CompilerParams(vmem_limit_bytes=50 * 2**20),
        cost_estimate=pl.CostEstimate(
            flops=2 * 27 * frames * rows * w_dev * channels * channels,
            bytes_accessed=8 * 2**20,
            transcendentals=2**20,
        ),
        name="conv",
    )(own0, own1, before, after, rim, rim_before, rim_after, left, right, gain, weight)


def permute(cells, axis, pairs):
    if cells.shape[-2] % 16:
        return lax.ppermute(cells, axis, pairs)
    flat = cells.reshape(-1, cells.shape[-1])
    return lax.ppermute(flat, axis, pairs).reshape(cells.shape)


def ends(cells, axis, dim, width):
    count = lax.axis_size(axis)
    head = lax.slice_in_dim(cells, 0, width, axis=dim)
    tail = lax.slice_in_dim(cells, cells.shape[dim] - width, cells.shape[dim], axis=dim)
    return (
        permute(tail, axis, [(i, i + 1) for i in range(count - 1)]),
        permute(head, axis, [(i + 1, i) for i in range(count - 1)]),
    )


def assemble_body(count, order, *refs):
    place = where()
    pieces, out, sems = refs[: 2 * len(order)], refs[-2], refs[-1]
    copies = []
    for i, d in enumerate(order):
        for kind in range(2):
            at = (place[5] + d) % count * 2 + (place[0] ^ kind)
            n = 2 * i + kind
            copies.append(pltpu.make_async_copy(pieces[n], out.at[at], sems.at[n]))
            copies[-1].start()
    for copy in copies:
        copy.wait()


def assemble(count, order, pieces):
    vmem = pl.BlockSpec(memory_space=pltpu.VMEM)
    return pl.pallas_call(
        functools.partial(assemble_body, count, order),
        out_shape=jax.ShapeDtypeStruct((len(pieces),) + pieces[0].shape, jnp.bfloat16),
        in_specs=[vmem] * len(pieces),
        out_specs=pl.BlockSpec(memory_space=pl.ANY),
        scratch_shapes=[pltpu.SemaphoreType.DMA((len(pieces),))],
        compiler_params=pltpu.CompilerParams(vmem_limit_bytes=4 * 2**20),
        name="assemble",
    )(*pieces)


def block_and_attention(latents, norm_gain, conv_weight, qkv_weight):
    _, _, w_dev, channels = latents.shape
    n_ta, n_ha, n_wa = lax.axis_size("ta"), lax.axis_size("ha"), lax.axis_size("wa")

    def everywhere(to):
        pairs = []
        for ta in range(n_ta):
            for ha in range(n_ha):
                for wa in range(n_wa):
                    dest = to(ta, ha, wa)
                    if dest is not None:
                        ta2, ha2, wa2 = dest
                        pairs.append(
                            ((ta * n_ha + ha) * n_wa + wa, (ta2 * n_ha + ha2) * n_wa + wa2)
                        )
        return pairs

    axes = ("ta", "ha", "wa")
    far_row, near_row, first, last, gain = faces(latents, norm_gain[None])
    odd = [(i, i + 1) for i in range(1, n_ha - 1, 2)]
    odd += [(j, i) for i, j in odd]
    rim_far = permute(far_row[:, None], "ha", odd)
    ups = [(i, i + 1) for i in range(n_ta - 1)]
    before = permute(last[None], "ta", ups)
    after = permute(first[None], "ta", [(j, i) for i, j in ups])
    rim_near = permute(near_row[:, None], "ha", [(i, i ^ 1) for i in range(n_ha)])
    rim = jnp.concatenate([rim_far, rim_near], axis=1)
    rim_before, rim_after = ends(rim, "ta", 0, 1)

    def side(at):
        return jnp.concatenate(
            [
                jnp.concatenate([x[:, :, at] for x in (before, first[None], last[None], after)], axis=0),
                jnp.concatenate([x[:, :, at] for x in (rim_before, rim, rim_after)], axis=0),
            ],
            axis=1,
        )

    left = permute(side(w_dev - 1), "wa", [(i, i + 1) for i in range(n_wa - 1)])
    right = permute(side(0), "wa", [(i + 1, i) for i in range(n_wa - 1)])
    mine = qkv_weight[:, 0].transpose(1, 0, 2)
    mine = permute(
        mine,
        axes,
        everywhere(
            lambda ta, ha, wa: (ta, ha, wa) if ha % 2 == wa % 2 else (ta, ha ^ 1, wa ^ 1)
        ),
    )
    weights = [mine] + [
        permute(mine, "ta", [(i, (i + d) % n_ta) for i in range(n_ta)])
        for d in range(1, n_ta)
    ]

    block_out, keep, give, edge = conv_block(
        first[None], last[None], before, after, rim, rim_before, rim_after, left, right,
        gain, conv_weight.reshape(9, 3 * channels, channels),
    )
    own = [keep] + [
        permute(give if d % 2 else keep, "wa", [(i, i ^ d) for i in range(n_wa)])
        for d in range(1, n_wa)
    ]
    other = [permute(x, "ha", [(j, j ^ 1) for j in range(n_ha)]) for x in own]

    edge = permute(edge, "ha", odd)
    rows_own = [edge[0]] + [
        permute(edge[d % 2], "wa", [(i, i ^ d) for i in range(n_wa)])
        for d in range(1, n_wa)
    ]
    rows_other = [permute(x, "ha", [(j, j ^ 1) for j in range(n_ha)]) for x in rows_own]
    slots = [project([(0, [own[i]], [other[i]])], weights)[0] for i in range(4)]
    heads, size = n_ta, qkv_weight.shape[3]
    inner = inner_heads(heads, size, slots)
    (halo,) = project([(1, rows_own, rows_other)], weights)
    pieces = []
    for d in range(heads - 1, -1, -1):
        out = one_head(d, size, slots, halo, inner)
        moved = permute(
            out,
            axes,
            everywhere(
                lambda ta, ha, wa: (
                    (ta - d) % n_ta,
                    ha - ha % 2 + wa % 2,
                    wa - wa % 2 + ha % 2,
                )
            ),
        )
        crossed = permute(moved[1], "ha", [(j, j ^ 1) for j in range(n_ha)])
        pieces += [moved[0], crossed]
    result = assemble(n_ta, list(range(heads - 1, -1, -1)), pieces)
    return block_out, result[:, :, :, None, :]


def solution(mesh):
    return jax.shard_map(
        block_and_attention,
        mesh=mesh,
        in_specs=(P("ta", "ha", "wa", None), P(), P(), P(None, ("ta", "wa"), None, None)),
        out_specs=(P("ta", "ha", "wa", None), P(None, "ha", None, ("ta", "wa"), None)),
        check_vma=False,
    )
```
